128 devices in a mesh: group: 4 (over x), rows: 32 (over z, y, core).
Axes of the slice: x: 4, y: 4, z: 4, core: 2. Of those that a mesh axis runs over, the one named last changes fastest.
Arguments:
- force_rows: float32 [6, 1048576], P(None, ('group', 'rows')), may hold values from -1.5 to 1.5
- owners: int32 [1048576, 1], P(('group', 'rows')), may hold values from 0 to 127; in each aligned block of 8192 rows (0 to 8191, 8192 to 16383, ...) at most 80 rows name the same one
- target: int32 [1048576], P(('group', 'rows')), may hold values from 0 to 255
- rbf_blocks: float32 [128, 256, 256], P(('group', 'rows')), may hold values from -0.375 to 0.375
- displacement: float32 [6, 32768], P(None, ('group', 'rows')), may hold values from -32 to 32
- u_basis: float32 [192, 6, 32768], P(None, None, ('group', 'rows')), may hold values from -3 to 3
- z_basis: float32 [192, 6, 32768], P(None, None, ('group', 'rows')), may hold values from -28 to 28
- v_new: float32 [32, 6, 32768], P(None, None, ('group', 'rows')), may hold values from -32 to 32
- w_new: float32 [32, 6, 32768], P(None, None, ('group', 'rows')), may hold values from -6 to 6
Outputs:
- u_restart: float32 [192, 6, 32768], P(None, None, ('group', 'rows'))
- z_restart: float32 [192, 6, 32768], P(None, None, ('group', 'rows'))
- next_disp: float32 [6, 32768], P(None, ('group', 'rows'))
- wetted_disp: float32 [6, 1048576], P(None, ('group', 'rows'))
The draws below stay inside these ranges and needn't reach their ends.
Inputs may be any that keep to these rules, and one draw needn't show every extreme that they name: `owners`: at most 80 of the face rows of one device name the same owner device, and some owner device is named by exactly 80 rows of one device in every draw.
All inputs are finite; a program needn't handle non-finite values.
Results may differ from the reference program's by a relative error of at most 0.00007.
Values sent between devices are 32-bit elements; how exact they have to be, the bound alone decides.
A program may use at most 64 MiB of HBM per device.

```python
import math
import jax
import jax.numpy as jnp
import numpy as np
from jax import lax

P_DEV = 256
FACES_DEV = 8192
BLK = 256
K = 192
M = 32
NPTS = 32768
FACES = 1048576
NBLK = 128
CAP = 80
N_GROUP = 4
N_ROWS = 32


def row_scale(key):
    place = jnp.arange(NPTS).astype(jnp.float32) / NPTS
    rough = jax.random.uniform(jax.random.fold_in(key, 13), (NPTS,), jnp.float32, 0.7, 1.4)
    return 10.0 ** (place - 0.5) * rough


def base_fields(key):
    scale = row_scale(key)
    fields = jax.random.truncated_normal(jax.random.fold_in(key, 11), -4.0, 4.0, (K, 6, NPTS), jnp.float32) * scale
    return (fields, scale)


def draw_z_basis(key, part):
    fields, scale = base_fields(key)
    return fields


def draw_v_new(key, part):
    fields, scale = base_fields(key)
    picked = fields[1:4 * M:4]
    noise = jax.random.truncated_normal(jax.random.fold_in(key, 14), -4.0, 4.0, (M, 6, NPTS), jnp.float32) * scale
    return 0.6 * picked + 0.8 * noise


def draw_displacement(key, part):
    fields, scale = base_fields(key)
    noise = jax.random.truncated_normal(jax.random.fold_in(key, 15), -4.0, 4.0, (6, NPTS), jnp.float32)
    return noise + 0.5 * (fields[2 * M + 1] - fields[K - 1])


def plant(values, own_key, smallest, largest):
    extent = values.shape
    spot = [jax.random.randint(jax.random.fold_in(own_key, axis), (), 0, extent[axis]) for axis in range(len(extent))]
    values = values.at[tuple(spot)].set(smallest)
    longest = extent.index(max(extent))
    spot[longest] = (spot[longest] + 1) % extent[longest]
    return values.at[tuple(spot)].set(largest)


def shard_levels(key, dims, shards, smallest, largest):
    level, own = 1.0, jax.random.fold_in(key, 6)
    for dim, parts in shards:
        draws = jnp.exp(jax.random.uniform(jax.random.fold_in(own, dim), (parts,), jnp.float32, smallest / len(shards), largest / len(shards)))
        level = level * jnp.repeat(draws, dims[dim] // parts).reshape([-1 if axis == dim else 1 for axis in range(len(dims))])
    return level


def assign_block(key, own, number, rows, count, top, most, skew):
    order = jax.random.permutation(key, count)
    packed, usual = shares(count, rows * top, most, skew, True), shares(count, rows * top, most, skew, False)
    places = jnp.arange(count)

    def named(sizes, offset_by):
        used = int((sizes > 0).sum())
        fixed = max(1, used // 4)
        shifted = fixed + (places - fixed + offset_by * (used - fixed)) % max(1, count - fixed)
        return jnp.zeros((count,), jnp.int32).at[order[jnp.where(places < fixed, places, shifted)]].set(jnp.asarray(sizes, jnp.int32))

    sizes = jnp.where(number % 4 == 0, named(packed, number // 4), named(usual, number - number // 4 - 1))
    mixed = jax.random.permutation(jax.random.fold_in(own, 3), count)
    giver, sink = mixed[0:count // 2 * 2:2], mixed[1:count // 2 * 2:2]
    room = jnp.minimum(sizes[giver] - 1, most - sizes[sink]) // 2
    room = jnp.where((giver == order[0]) | (sink == order[0]) | (sizes[sink] == 0), 0, jnp.maximum(room, 0))
    shifted = jax.random.randint(jax.random.fold_in(own, 4), (count // 2,), 0, 1 << 20) % (room + 1)
    sizes = sizes.at[giver].add(-shifted).at[sink].add(shifted)
    items = jnp.searchsorted(jnp.cumsum(sizes), jnp.arange(rows * top), side="right").astype(jnp.int32)
    grid = items.reshape(top, rows).T
    grid = grid[jax.random.permutation(jax.random.fold_in(own, 1), rows)]
    offset_by = jax.random.randint(jax.random.fold_in(own, 2), (rows, 1), 0, top)
    return jnp.take_along_axis(grid, (jnp.arange(top)[None, :] + offset_by) % top, axis=1)


def shares(number_of, total, limit, slope, full):
    weights = [(1 << 20) // math.isqrt(standing ** slope) + 1 for standing in range(1, number_of + 1)]
    largest = limit if full else min(limit, max(-(-total // number_of), total * weights[0] // sum(weights)))
    least = 1 if total - largest >= number_of - 1 else 0
    counts, rest = [largest] + [least] * (number_of - 1), total - largest - least * (number_of - 1)
    while rest > 0:
        free = [i for i in range(1, number_of) if counts[i] < largest] or [i for i in range(1, number_of) if counts[i] < limit]
        pool, remaining = sum([weights[i] for i in free]), rest
        for i in free:
            extra = min(limit - counts[i], max(1, remaining * weights[i] // pool), rest)
            counts[i] = counts[i] + extra
            rest = rest - extra
    return np.array(counts)


def scatter_about(key, dims, width, reach, split=(), kind=jnp.bfloat16):
    factor_of = shard_levels(key, dims, split, -0.22, 0.18) if split else 1.0
    values = jax.random.normal(key, dims, jnp.float32) * width * factor_of
    return jnp.minimum(jnp.maximum(values, -reach), reach).astype(kind)


def setup_inputs(seed: int = 0) -> dict:
    streams_of = jax.random.split(jax.random.key(seed), 10)
    force_rows = scatter_about(streams_of[0], (6, FACES), 0.25, 1.5, ((1, 128),), jnp.float32)
    owners_keys = jax.random.split(jax.random.fold_in(streams_of[1], 1), FACES // FACES_DEV)
    owners_turns = jax.random.permutation(jax.random.fold_in(streams_of[1], 3), FACES // FACES_DEV)
    owners = jax.vmap(lambda own, number: assign_block(jax.random.fold_in(streams_of[1], 2), own, number, FACES_DEV, N_GROUP * N_ROWS, 1, CAP, 1))(owners_keys, owners_turns).reshape((FACES, 1))
    target = plant(jax.random.randint(streams_of[2], (FACES,), 0, P_DEV), jax.random.fold_in(streams_of[2], 1), 0, P_DEV - 1).astype(jnp.int32)
    rbf_blocks = scatter_about(streams_of[3], (NBLK, BLK, BLK), BLK ** -0.5, 0.375, ((0, 128),), jnp.float32)
    displacement = draw_displacement(jax.random.fold_in(streams_of[9], 71), 0)
    u_basis = scatter_about(streams_of[5], (K, 6, NPTS), 0.5, 3.0, ((2, 128),), jnp.float32)
    z_basis = draw_z_basis(jax.random.fold_in(streams_of[9], 71), 0)
    v_new = draw_v_new(jax.random.fold_in(streams_of[9], 71), 0)
    w_new = scatter_about(streams_of[8], (M, 6, NPTS), 1.0, 6.0, ((2, 128),), jnp.float32)
    return dict(force_rows=force_rows, owners=owners, target=target, rbf_blocks=rbf_blocks, displacement=displacement, u_basis=u_basis, z_basis=z_basis, v_new=v_new, w_new=w_new)


precise = lax.Precision.HIGHEST

def reference(force_rows, owners, target, rbf_blocks, displacement, u_basis, z_basis, v_new, w_new):
    points_all = displacement.shape[1]
    dof_total = 6 * points_all
    point_idx = (owners[:, 0] * P_DEV + target).astype(jnp.int32)
    point_load = jnp.zeros((6, points_all), jnp.float32).at[:, point_idx].add(force_rows)
    blocks = point_load.reshape(6, points_all // BLK, BLK)
    response = jnp.einsum('cbi,bij->cbj', blocks, rbf_blocks, precision=precise).reshape(6, points_all)
    residual = response - displacement
    u_flat = u_basis.reshape(K, dof_total)
    z_flat = z_basis.reshape(K, dof_total)
    v_flat = v_new.reshape(M, dof_total)
    w_flat = w_new.reshape(M, dof_total)
    r_flat = residual.reshape(dof_total)
    cross_new = jnp.dot(z_flat, v_flat.T, precision=precise) / dof_total
    gram_new = jnp.dot(v_flat, v_flat.T, precision=precise) / dof_total
    chol_new = jnp.linalg.cholesky(gram_new)
    new_cols = jax.scipy.linalg.cho_solve((chol_new, True), v_flat)
    jac_v = jnp.dot(cross_new.T, u_flat, precision=precise)
    u_joined = jnp.concatenate([u_flat[M:], w_flat - jac_v], 0)
    z_joined = jnp.concatenate([z_flat[M:], new_cols], 0)
    gram_rest = jnp.dot(z_joined, z_joined.T, precision=precise) / dof_total
    chol_rest = jnp.linalg.cholesky(gram_rest)
    u_restart = jnp.dot(chol_rest.T, u_joined, precision=precise)
    z_restart = jax.scipy.linalg.solve_triangular(chol_rest, z_joined, lower=True)
    step_coef = jnp.dot(z_restart, r_flat, precision=precise) / dof_total
    next_disp = response + jnp.dot(step_coef, u_restart, precision=precise).reshape(6, points_all)
    wetted_disp = next_disp[:, point_idx]
    return (u_restart.reshape(K, 6, points_all), z_restart.reshape(K, 6, points_all), next_disp, wetted_disp)
```

```python
import functools

import jax
import jax.numpy as jnp
from jax import lax
from jax.experimental import pallas as pl
from jax.experimental.pallas import tpu as pltpu
from jax.sharding import PartitionSpec as P

BLK = 256
K = 192
M = 32
KEEP = K - M
NB = 32
ROWS = K + M
GBLK = ROWS // 8
FACE_CHUNK = 512

MESH = pl.DeviceIdType.MESH
F32 = jnp.float32
BF16 = jnp.bfloat16
AXES = ("group", "rows")


def iota(shape, dim):
    return lax.broadcasted_iota(jnp.int32, shape, dim)


def dot(a, b, dims):
    return lax.dot_general(
        a, b, (dims, ((), ())), precision=lax.Precision.HIGHEST, preferred_element_type=F32
    )


def nn(a, b):
    return dot(a, b, ((1,), (0,)))


def nt(a, b):
    return dot(a, b, ((1,), (1,)))


def tn(a, b):
    return dot(a, b, ((0,), (0,)))


def split(x):
    high = x.astype(BF16)
    return high, (x - high.astype(F32)).astype(BF16)


def eliminate(panel, first):
    rows = iota((NB, 1), 0)
    for j in range(NB):
        at = first + j
        pivot_row = panel[j : j + 1, :]
        inverse = 1.0 / pivot_row[:, at : at + 1]
        factor = jnp.where(rows > j, panel[:, at : at + 1] * inverse, 0.0)
        panel = panel - factor * pivot_row
    own = iota(panel.shape, 1) == first + iota(panel.shape, 0)
    pivots = jnp.sum(jnp.where(own, panel, 0.0), axis=1, keepdims=True)
    return panel * lax.rsqrt(pivots)


def exchange_kernel(
    n_g, n_r,
    force, owner, target, rbf, disp, u, z, v, w,
    table_hi, table_lo, mix_u, mix_z, next_disp,
    gram_send, gram_recv, gram_sum, gram_all,
    load, load_recv, q_send, q_recv, disp_send, table,
    aug, coef_scr,
    gs_sem, gr_sem, ga_send_sem, ga_sem, ls_sem, lr_sem, qs_sem, qr_sem, ts_sem, tr_sem,
):
    n = n_g * n_r
    me = lax.axis_index("group") * n_r + lax.axis_index("rows")
    reducers = min(n, GBLK)
    stride = n // 32 if n >= 32 else 1
    slots = -(-GBLK // reducers)
    dof_total = 6 * BLK * n

    def device(p):
        return (p // n_r, lax.rem(p, n_r))

    def others(body):
        def step(k, carry):
            body(lax.rem(me + k, n))
            return carry

        lax.fori_loop(1, n, step, 0)

    def remote(src, dst, send, recv, p):
        return pltpu.make_async_remote_copy(
            src_ref=src, dst_ref=dst, send_sem=send, recv_sem=recv,
            device_id=device(p), device_id_type=MESH,
        )

    barrier = pltpu.get_barrier_semaphore()
    others(lambda p: pl.semaphore_signal(barrier, inc=1, device_id=device(p), device_id_type=MESH))

    gram = jnp.zeros((ROWS, ROWS), F32)
    for c in range(6):
        joined = jnp.concatenate([z[c, M:, :], v[c], z[c, :M, :]], 0)
        gram = gram + nt(joined, joined)
    gram = gram * (1.0 / dof_total)
    gram = jnp.concatenate([gram, jnp.zeros((ROWS, 256 - ROWS), F32)], 1)
    gram_send[...] = gram.reshape(GBLK, 8, 256)

    pl.semaphore_wait(barrier, n - 1)

    def gram_blocks(away, here):
        def step(b, carry):
            slot, p = b // reducers, lax.rem(b, reducers) * stride

            @pl.when(p != me)
            def _():
                away(b, slot, p)

            if here is not None:

                @pl.when(p == me)
                def _():
                    here(b, slot)

            return carry

        lax.fori_loop(0, GBLK, step, 0)

    def gram_copy(b, slot, p):
        return remote(gram_send.at[b], gram_recv.at[slot, me], gs_sem, gr_sem.at[slot], p)

    gram_blocks(
        lambda b, slot, p: gram_copy(b, slot, p).start(),
        lambda b, slot: pltpu.make_async_copy(
            gram_send.at[b], gram_recv.at[slot, me], gr_sem.at[slot]
        ).start(),
    )

    def reducing(body):
        for slot in range(slots):
            b = slot * reducers + me // stride

            @pl.when((lax.rem(me, stride) == 0) & (me // stride < reducers) & (b < GBLK))
            def _():
                body(slot, b)

    faces = force.shape[1]
    chunk = min(FACE_CHUNK, faces)
    load[...] = jnp.zeros_like(load)

    def scatter(i, carry):
        at = pl.ds(pl.multiple_of(i * chunk, chunk), chunk)
        at_owner = (iota((n, chunk), 0) == owner[:, at]).astype(F32).astype(BF16)
        at_point = (iota((BLK, chunk), 0) == target[:, at]).astype(F32).astype(BF16)
        high, low = split(force[:, at])
        left = jnp.concatenate(
            [
                jnp.concatenate([at_owner * high[c : c + 1], at_owner * low[c : c + 1]], 1)
                for c in range(6)
            ],
            0,
        )
        right = jnp.concatenate([at_point, at_point], 1)
        add = lax.dot_general(left, right, (((1,), (1,)), ((), ())), preferred_element_type=F32)
        load[...] += add.reshape(6, n, BLK)
        return carry

    half = faces // chunk // 2
    lax.fori_loop(0, half, scatter, 0)

    def reduce_gram(slot, b):
        pltpu.make_async_copy(gram_recv.at[slot], gram_recv.at[slot], gr_sem.at[slot]).wait()
        gram_sum[slot] = jnp.sum(gram_recv[slot], axis=0)

    reducing(reduce_gram)

    def share_gram(slot, b):
        others(lambda p: remote(gram_sum.at[slot], gram_all.at[b], ga_send_sem, ga_sem, p).start())
        pltpu.make_async_copy(gram_sum.at[slot], gram_all.at[b], ga_sem).start()

    reducing(share_gram)

    lax.fori_loop(half, faces // chunk, scatter, 0)

    def row(ref, p):
        return ref.at[:, pl.ds(p, 1), :]

    def load_copy(p):
        return remote(row(load, p), row(load_recv, me), ls_sem, lr_sem, p)

    others(lambda p: load_copy(p).start())
    pltpu.make_async_copy(row(load, me), row(load_recv, me), lr_sem).start()

    pltpu.make_async_copy(gram_all, gram_all, ga_sem).wait()
    total = gram_all[...].reshape(ROWS, 256)

    lane32 = iota((NB, 128), 1)
    row32 = iota((NB, 128), 0)
    start = jnp.where(
        (lane32 >= 32) & (lane32 < 64), total[KEEP:K, 128:], jnp.where(lane32 - 64 == row32, 1.0, 0.0)
    )
    factor = eliminate(start, 32)
    factor = pltpu.roll(factor, 96, 1)
    factor = jnp.where((lane32 >= 32) & (lane32 < 64), factor, 0.0)
    inverse = tn(factor, factor)
    scaled = nn(total[:, 128:], inverse)

    lanes = iota((ROWS, 256), 1)
    index = iota((ROWS, 256), 0)
    new_lane = (lanes >= KEEP) & (lanes < K)
    new_row = (index >= KEEP) & (index < K)
    scaled = jnp.concatenate([jnp.zeros((ROWS, 128), F32), scaled], 1)
    inverse_rows = jnp.concatenate(
        [jnp.zeros((KEEP, 128), F32), inverse[32:64], jnp.zeros((M, 128), F32)], 0
    )
    inverse_full = jnp.concatenate([jnp.zeros((ROWS, 128), F32), inverse_rows], 1)
    unit = jnp.where(lanes == index, 1.0, 0.0)
    matrix = jnp.where(new_lane, jnp.where(new_row, inverse_full, scaled), total)
    matrix = jnp.where(lanes < K, matrix, 0.0)
    extra = jnp.where(new_lane, inverse_full, unit)
    aug[:, 0:256] = matrix[:K]
    aug[:, 256:512] = extra[:K]
    coef = jnp.where(new_lane, jnp.where(new_row, inverse_full, -scaled), jnp.where(lanes < KEEP, unit, 0.0))
    coef_scr[...] = coef
    change = jnp.where(lanes == index, 1.0, jnp.where(new_row & (lanes < ROWS), -total, 0.0))
    change = jnp.where(new_row & new_lane, unit, change)
    change = jnp.where(index < K, change, 0.0)

    def block(b):
        r0 = b * NB
        panel = aug[r0 : r0 + NB, :]
        lane = iota((NB, 512), 1)
        done = eliminate(panel, r0)
        done = jnp.where(lane < r0, 0.0, done)
        aug[r0 : r0 + NB, :] = done
        if r0 + NB < K:
            first = 128 if r0 + NB >= 128 else 0
            update = tn(done[:, first:256], done)
            aug[r0 + NB : K, :] = aug[r0 + NB : K, :] - update[r0 + NB - first : K - first, :]

    block(0)
    block(1)

    pltpu.make_async_copy(load_recv, load_recv, lr_sem).wait()
    point_load = jnp.concatenate(
        [jnp.sum(load_recv[c], axis=0, keepdims=True) for c in range(6)], 0
    )
    response = nn(point_load, rbf[...])
    residual = response - disp[...]
    disp_send[...] = response.reshape(6, 1, BLK)
    weighted = jnp.zeros((K, BLK), F32)
    for c in range(6):
        kept = jnp.concatenate([z[c, M:, :], v[c]], 0)
        weighted = weighted + kept * residual[c : c + 1]
    q_column = jnp.sum(weighted, axis=1, keepdims=True) * (1.0 / dof_total)
    diagonal = iota((K, 256), 0) == iota((K, 256), 1)
    q_send[...] = jnp.sum(jnp.where(diagonal, q_column, 0.0), axis=0, keepdims=True)

    def q_copy(p):
        return remote(q_send, q_recv.at[me], qs_sem, qr_sem, p)

    others(lambda p: q_copy(p).start())
    pltpu.make_async_copy(q_send, q_recv.at[me], qr_sem).start()

    block(2)
    block(3)

    pltpu.make_async_copy(q_recv, q_recv, qr_sem).wait()
    q_row = jnp.sum(q_recv[...], axis=0)
    step_coef = jnp.sum(coef_scr[...] * q_row, axis=1, keepdims=True)
    for c in range(6):
        joined = jnp.concatenate([u[c, M:, :], w[c], u[c, :M, :]], 0)
        disp_send[c] = disp_send[c] + jnp.sum(joined * step_coef, axis=0, keepdims=True)
        next_disp[c : c + 1, :] = disp_send[c]

    def table_copy(p):
        return remote(disp_send, row(table, me), ts_sem, tr_sem, p)

    others(lambda p: table_copy(p).start())
    pltpu.make_async_copy(disp_send, row(table, me), tr_sem).start()

    block(4)
    block(5)

    upper = jnp.where(iota((K, 256), 1) >= iota((K, 256), 0), aug[:, 0:256], 0.0)
    mix_u[...] = nn(upper[:, :K], change[:K])
    mix_z[...] = aug[:, 256:512]

    pltpu.make_async_copy(table, table, tr_sem).wait()
    for c in range(6):
        high, low = split(table[c])
        table_hi[c * n : (c + 1) * n, :] = high
        table_lo[c * n : (c + 1) * n, :] = low

    gram_blocks(lambda b, slot, p: gram_copy(b, slot, p).wait_send(), None)
    reducing(
        lambda slot, b: others(
            lambda p: remote(
                gram_sum.at[slot], gram_all.at[b], ga_send_sem, ga_sem, p
            ).wait_send()
        )
    )
    others(lambda p: load_copy(p).wait_send())
    others(lambda p: q_copy(p).wait_send())
    others(lambda p: table_copy(p).wait_send())


def finish_kernel(
    n, owner, target, table_hi, table_lo, mix_u, mix_z, u, z, v, w,
    u_out, z_out, wetted, u_buf, z_buf, sem,
):
    left_u = mix_u[:, :ROWS]
    left_z = mix_z[:, :K]
    for c in range(6):
        u_buf[c] = nn(left_u, jnp.concatenate([u[c, M:, :], w[c], u[c, :M, :]], 0))
        z_buf[c] = nn(left_z, jnp.concatenate([z[c, M:, :], v[c]], 0))
    u_copy = pltpu.make_async_copy(u_buf, u_out, sem.at[0])
    z_copy = pltpu.make_async_copy(z_buf, z_out, sem.at[1])
    u_copy.start()
    z_copy.start()

    faces = wetted.shape[1]
    chunk = min(FACE_CHUNK, faces)
    left = jnp.concatenate([table_hi[...], table_lo[...]], 1)

    def gather(i, carry):
        at = pl.ds(pl.multiple_of(i * chunk, chunk), chunk)
        at_owner = iota((n, chunk), 0) == owner[:, at]
        at_point = (iota((BLK, chunk), 0) == target[:, at]).astype(F32).astype(BF16)
        right = jnp.concatenate([at_point, at_point], 0)
        values = lax.dot_general(left, right, (((1,), (0,)), ((), ())), preferred_element_type=F32)
        rows = [
            jnp.sum(jnp.where(at_owner, values[c * n : (c + 1) * n], 0.0), axis=0, keepdims=True)
            for c in range(6)
        ]
        wetted[:, at] = jnp.concatenate(rows, 0)
        return carry

    lax.fori_loop(0, faces // chunk, gather, 0)
    u_copy.wait()
    z_copy.wait()


def on_device(n_g, n_r, force_rows, owners, target, rbf_blocks, displacement, u_basis, z_basis, v_new, w_new):
    n = n_g * n_r
    faces = force_rows.shape[1]
    reducers = min(n, GBLK)
    slots = -(-GBLK // reducers)
    owner = owners.reshape(1, faces)
    point = target.reshape(1, faces)
    u, z, v, w = (x.transpose(1, 0, 2) for x in (u_basis, z_basis, v_new, w_new))
    vmem = pl.BlockSpec(memory_space=pltpu.VMEM)
    table_hi, table_lo, mix_u, mix_z, next_disp = pl.pallas_call(
        functools.partial(exchange_kernel, n_g, n_r),
        out_shape=(
            jax.ShapeDtypeStruct((6 * n, BLK), BF16),
            jax.ShapeDtypeStruct((6 * n, BLK), BF16),
            jax.ShapeDtypeStruct((K, 256), F32),
            jax.ShapeDtypeStruct((K, 256), F32),
            jax.ShapeDtypeStruct((6, BLK), F32),
        ),
        in_specs=[vmem] * 9,
        out_specs=(vmem,) * 5,
        scratch_shapes=[
            pltpu.VMEM((GBLK, 8, 256), F32),
            pltpu.VMEM((slots, n, 8, 256), F32),
            pltpu.VMEM((slots, 8, 256), F32),
            pltpu.VMEM((GBLK, 8, 256), F32),
            pltpu.VMEM((6, n, BLK), F32),
            pltpu.VMEM((6, n, BLK), F32),
            pltpu.VMEM((1, 256), F32),
            pltpu.VMEM((n, 1, 256), F32),
            pltpu.VMEM((6, 1, BLK), F32),
            pltpu.VMEM((6, n, BLK), F32),
            pltpu.VMEM((K, 512), F32),
            pltpu.VMEM((ROWS, 256), F32),
            pltpu.SemaphoreType.DMA,
            pltpu.SemaphoreType.DMA((slots,)),
            pltpu.SemaphoreType.DMA,
            pltpu.SemaphoreType.DMA,
            pltpu.SemaphoreType.DMA,
            pltpu.SemaphoreType.DMA,
            pltpu.SemaphoreType.DMA,
            pltpu.SemaphoreType.DMA,
            pltpu.SemaphoreType.DMA,
            pltpu.SemaphoreType.DMA,
        ],
        compiler_params=pltpu.CompilerParams(collective_id=0, has_side_effects=True),
        name="exchange",
    )(force_rows, owner, point, rbf_blocks[0], displacement, u, z, v, w)
    u_out, z_out, wetted = pl.pallas_call(
        functools.partial(finish_kernel, n),
        out_shape=(
            jax.ShapeDtypeStruct((6, K, BLK), F32),
            jax.ShapeDtypeStruct((6, K, BLK), F32),
            jax.ShapeDtypeStruct((6, faces), F32),
        ),
        in_specs=[vmem] * 10,
        out_specs=(
            pl.BlockSpec(memory_space=pl.ANY),
            pl.BlockSpec(memory_space=pl.ANY),
            vmem,
        ),
        scratch_shapes=[
            pltpu.VMEM((6, K, BLK), F32),
            pltpu.VMEM((6, K, BLK), F32),
            pltpu.SemaphoreType.DMA((2,)),
        ],
        name="finish",
    )(owner, point, table_hi, table_lo, mix_u, mix_z, u, z, v, w)
    return u_out.transpose(1, 0, 2), z_out.transpose(1, 0, 2), next_disp, wetted


def solution(mesh):
    return jax.shard_map(
        functools.partial(on_device, mesh.shape["group"], mesh.shape["rows"]),
        mesh=mesh,
        in_specs=(
            P(None, AXES),
            P(AXES, None),
            P(AXES),
            P(AXES, None, None),
            P(None, AXES),
            P(None, None, AXES),
            P(None, None, AXES),
            P(None, None, AXES),
            P(None, None, AXES),
        ),
        out_specs=(P(None, None, AXES), P(None, None, AXES), P(None, AXES), P(None, AXES)),
        check_vma=False,
    )
```

```python
import functools

import jax
import jax.numpy as jnp
from jax import lax
from jax.experimental import pallas as pl
from jax.experimental.pallas import tpu as pltpu
from jax.sharding import PartitionSpec as P

BLK = 256
K = 192
M = 32
KEEP = K - M
NB = 32
ROWS = K + M
GBLK = ROWS // 8
FACE_CHUNK = 2048
GATHER_CHUNK = 1024
UNROLL = 8

MESH = pl.DeviceIdType.MESH
F32 = jnp.float32
BF16 = jnp.bfloat16
AXES = ("group", "rows")


def iota(shape, dim):
    return lax.broadcasted_iota(jnp.int32, shape, dim)


def dot(a, b, dims):
    return lax.dot_general(
        a, b, (dims, ((), ())), precision=lax.Precision.HIGHEST, preferred_element_type=F32
    )


def nn(a, b):
    return dot(a, b, ((1,), (0,)))


def nt(a, b):
    return dot(a, b, ((1,), (1,)))


def tn(a, b):
    return dot(a, b, ((0,), (0,)))


def split(x):
    high = x.astype(BF16)
    return high, (x - high.astype(F32)).astype(BF16)


def eliminate(tiles, first):
    rows = iota((NB, 128), 0)
    tiles = list(tiles)
    base = first // 128
    for j in range(0, NB, 4):
        lane = first % 128 + j
        pivot_tile = tiles[base]
        c = [jnp.broadcast_to(pivot_tile[:, lane + i : lane + i + 1], (NB, 128)) for i in range(4)]
        a = {
            (i, k): jnp.broadcast_to(c[k][j + i : j + i + 1, :], (NB, 128))
            for i in range(4)
            for k in range(i, 4)
        }
        p0 = 1.0 / a[0, 0]
        l1, l2, l3 = a[0, 1] * p0, a[0, 2] * p0, a[0, 3] * p0
        b11, b12, b13 = a[1, 1] - l1 * a[0, 1], a[1, 2] - l1 * a[0, 2], a[1, 3] - l1 * a[0, 3]
        b22, b23, b33 = a[2, 2] - l2 * a[0, 2], a[2, 3] - l2 * a[0, 3], a[3, 3] - l3 * a[0, 3]
        p1 = 1.0 / b11
        l21, l31 = b12 * p1, b13 * p1
        b22, b23, b33 = b22 - l21 * b12, b23 - l21 * b13, b33 - l31 * b13
        p2 = 1.0 / b22
        l32 = b23 * p2
        p3 = 1.0 / (b33 - l32 * b23)
        m0 = jnp.where(rows > j, c[0] * p0, 0.0)
        m1 = jnp.where(rows > j + 1, (c[1] - m0 * a[0, 1]) * p1, 0.0)
        m2 = jnp.where(rows > j + 2, (c[2] - m0 * a[0, 2] - m1 * b12) * p2, 0.0)
        m3 = jnp.where(rows > j + 3, (c[3] - m0 * a[0, 3] - m1 * b13 - m2 * b23) * p3, 0.0)
        m2 = m2 - m3 * l32
        m1 = m1 - m2 * l21 - m3 * l31
        m0 = m0 - m1 * l1 - m2 * l2 - m3 * l3
        for t, tile in enumerate(tiles):
            r = [tile[j + i : j + i + 1, :] for i in range(4)]
            tiles[t] = tile - (m0 * r[0] + m1 * r[1]) - (m2 * r[2] + m3 * r[3])
    own = iota((NB, 128), 1) == first % 128 + rows
    pivots = jnp.sum(jnp.where(own, tiles[base], 0.0), axis=1, keepdims=True)
    scale = lax.rsqrt(pivots)
    return [tile * scale for tile in tiles]
def exchange_kernel(
    n_g, n_r,
    force, owner, target, rbf_any, disp_any, u_any, z_any, v_any, w_any,
    table_hi, table_lo, mix_u, mix_z, next_disp,
    rbf, disp, u, z, v, w,
    gram_send, gram_recv, gram_sum, gram_all,
    load_pair, load_own, pair_recv, load_recv, q_send, q_recv, disp_send, table_own, table_pair,
    aug, coef_scr,
    in_sem, gs_sem, gr_sem, ga_send_sem, ga_sem, ps_sem, pr_sem, ls_sem, lr_sem,
    qs_sem, qr_sem, ts_sem, tr_sem, fs_sem, fr_sem,
):
    n = n_g * n_r
    half = n // 2
    me = lax.axis_index("group") * n_r + lax.axis_index("rows")
    chip, core = me // 2, lax.rem(me, 2)
    reducers = min(n, GBLK)
    stride = n // 32 if n >= 32 else 1
    slots = -(-GBLK // reducers)
    dof_total = 6 * BLK * n

    def device(p):
        return (p // n_r, lax.rem(p, n_r))

    def others(body, unroll=1):
        def step(k, carry):
            body(lax.rem(me + k, n))
            return carry

        lax.fori_loop(1, n, step, 0, unroll=unroll)

    def other_chips(body, unroll=1):
        def step(k, carry):
            body(lax.rem(chip + k, half))
            return carry

        lax.fori_loop(1, half, step, 0, unroll=unroll)

    def remote(src, dst, send, recv, p):
        return pltpu.make_async_remote_copy(
            src_ref=src, dst_ref=dst, send_sem=send, recv_sem=recv,
            device_id=device(p), device_id_type=MESH,
        )

    loads = [
        pltpu.make_async_copy(src, dst, in_sem.at[i])
        for i, (src, dst) in enumerate(
            ((z_any, z), (v_any, v), (rbf_any, rbf), (disp_any, disp), (u_any, u), (w_any, w))
        )
    ]
    for copy in loads:
        copy.start()
    barrier = pltpu.get_barrier_semaphore()
    others(
        lambda p: pl.semaphore_signal(barrier, inc=1, device_id=device(p), device_id_type=MESH),
        UNROLL,
    )

    loads[0].wait()
    loads[1].wait()
    gram = jnp.zeros((ROWS, ROWS), F32)
    for c in range(6):
        joined = jnp.concatenate([z[c, M:, :], v[c], z[c, :M, :]], 0)
        gram = gram + nt(joined, joined)
    gram = gram * (1.0 / dof_total)
    gram = jnp.concatenate([gram, jnp.zeros((ROWS, 256 - ROWS), F32)], 1)
    gram_send[...] = gram.reshape(GBLK, 8, 256)

    faces = force.shape[1]
    chunk = min(FACE_CHUNK, faces)

    def scatter_to(load, parity):
        def scatter(i, carry):
            at = pl.ds(pl.multiple_of(i * chunk, chunk), chunk)
            named = iota((half, chunk), 0) * 2 + parity
            at_owner = (named == owner[:, at]).astype(F32).astype(BF16)
            at_point = (iota((BLK, chunk), 0) == target[:, at]).astype(F32).astype(BF16)
            high, low = split(force[:, at])
            left = jnp.concatenate(
                [
                    jnp.concatenate([at_owner * high[c : c + 1], at_owner * low[c : c + 1]], 1)
                    for c in range(6)
                ],
                0,
            )
            right = jnp.concatenate([at_point, at_point], 1)
            add = lax.dot_general(
                left, right, (((1,), (1,)), ((), ())), preferred_element_type=F32
            )
            load[...] += add.reshape(6, half, BLK)
            return carry

        load[...] = jnp.zeros_like(load)
        lax.fori_loop(0, faces // chunk, scatter, 0)

    scatter_to(load_pair, 1 - core)

    pl.semaphore_wait(barrier, n - 1)

    def gram_blocks(away, here):
        def step(b, carry):
            slot, p = b // reducers, lax.rem(b, reducers) * stride

            @pl.when(p != me)
            def _():
                away(b, slot, p)

            if here is not None:

                @pl.when(p == me)
                def _():
                    here(b, slot)

            return carry

        lax.fori_loop(0, GBLK, step, 0)

    def gram_copy(b, slot, p):
        return remote(gram_send.at[b], gram_recv.at[slot, me], gs_sem, gr_sem.at[slot], p)

    gram_blocks(
        lambda b, slot, p: gram_copy(b, slot, p).start(),
        lambda b, slot: pltpu.make_async_copy(
            gram_send.at[b], gram_recv.at[slot, me], gr_sem.at[slot]
        ).start(),
    )
    partner = 2 * chip + 1 - core
    pair_copy = remote(load_pair, pair_recv, ps_sem, pr_sem, partner)
    pair_copy.start()

    scatter_to(load_own, core)

    pair_copy.wait_recv()
    load_own[...] += pair_recv[...]

    def row(ref, p):
        return ref.at[:, pl.ds(p, 1), :]

    def load_copy(p):
        return remote(row(load_own, p), row(load_recv, chip), ls_sem, lr_sem, 2 * p + core)

    other_chips(lambda p: load_copy(p).start(), UNROLL)
    pltpu.make_async_copy(row(load_own, chip), row(load_recv, chip), lr_sem).start()

    def reducing(body):
        for slot in range(slots):
            b = slot * reducers + me // stride

            @pl.when((lax.rem(me, stride) == 0) & (me // stride < reducers) & (b < GBLK))
            def _():
                body(slot, b)

    def reduce_gram(slot, b):
        pltpu.make_async_copy(gram_recv.at[slot], gram_recv.at[slot], gr_sem.at[slot]).wait()
        gram_sum[slot] = jnp.sum(gram_recv[slot], axis=0)

    reducing(reduce_gram)

    def share_copy(slot, b, p):
        return remote(gram_sum.at[slot], gram_all.at[b], ga_send_sem, ga_sem, p)

    def share_gram(slot, b):
        others(lambda p: share_copy(slot, b, p).start(), UNROLL)
        pltpu.make_async_copy(gram_sum.at[slot], gram_all.at[b], ga_sem).start()

    reducing(share_gram)
    for copy in loads[2:]:
        copy.wait()

    pltpu.make_async_copy(load_recv, load_recv, lr_sem).wait()
    point_load = jnp.concatenate(
        [jnp.sum(load_recv[c], axis=0, keepdims=True) for c in range(6)], 0
    )
    response = nn(point_load, rbf[...])
    residual = response - disp[...]
    disp_send[...] = response.reshape(6, 1, BLK)
    weighted = jnp.zeros((K, BLK), F32)
    for c in range(6):
        kept = jnp.concatenate([z[c, M:, :], v[c]], 0)
        weighted = weighted + kept * residual[c : c + 1]
    q_column = jnp.sum(weighted, axis=1, keepdims=True) * (1.0 / dof_total)
    diagonal = iota((K, 256), 0) == iota((K, 256), 1)
    q_send[...] = jnp.sum(jnp.where(diagonal, q_column, 0.0), axis=0, keepdims=True)

    def q_copy(p):
        return remote(q_send, q_recv.at[me], qs_sem, qr_sem, p)

    others(lambda p: q_copy(p).start(), UNROLL)
    pltpu.make_async_copy(q_send, q_recv.at[me], qr_sem).start()

    pltpu.make_async_copy(gram_all, gram_all, ga_sem).wait()
    total = gram_all[...].reshape(ROWS, 256)

    lane32 = iota((NB, 128), 1)
    row32 = iota((NB, 128), 0)
    middle = (lane32 >= 32) & (lane32 < 64)
    start = jnp.where(middle, total[KEEP:K, 128:], jnp.where(lane32 - 64 == row32, 1.0, 0.0))
    factor = pltpu.roll(eliminate([start], 32)[0], 96, 1)
    factor = jnp.where(middle, factor, 0.0)
    inverse = tn(factor, factor)
    scaled = nn(total[:, 128:], inverse)

    lanes = iota((ROWS, 256), 1)
    index = iota((ROWS, 256), 0)
    new_lane = (lanes >= KEEP) & (lanes < K)
    new_row = (index >= KEEP) & (index < K)
    scaled = jnp.concatenate([jnp.zeros((ROWS, 128), F32), scaled], 1)
    inverse_rows = jnp.concatenate(
        [jnp.zeros((KEEP, 128), F32), inverse[32:64], jnp.zeros((M, 128), F32)], 0
    )
    inverse_full = jnp.concatenate([jnp.zeros((ROWS, 128), F32), inverse_rows], 1)
    unit = jnp.where(lanes == index, 1.0, 0.0)
    matrix = jnp.where(new_lane, jnp.where(new_row, inverse_full, scaled), total)
    matrix = jnp.where(lanes < K, matrix, 0.0)
    extra = jnp.where(new_lane, inverse_full, unit)
    aug[:, 0:256] = matrix[:K]
    aug[:, 256:512] = extra[:K]
    coef_scr[...] = jnp.where(
        new_lane,
        jnp.where(new_row, inverse_full, -scaled),
        jnp.where(lanes < KEEP, unit, 0.0),
    )
    change = jnp.where(lanes == index, 1.0, jnp.where(new_row & (lanes < ROWS), -total, 0.0))
    change = jnp.where(new_row & new_lane, unit, change)[:K]

    def tile(t):
        return slice(t * 128, t * 128 + 128)

    def block(b):
        r0, after = b * NB, b * NB + NB
        rows = slice(r0, after)
        active = [0, 1, 2] if after <= 128 else [1, 2, 3]
        done = eliminate([aug[rows, tile(t)] for t in active], r0 - 128 * active[0])
        lane = iota((NB, 128), 1)
        for i, t in enumerate(active):
            if t < 2:
                done[i] = jnp.where(lane + t * 128 < r0, 0.0, done[i])
            aug[rows, tile(t)] = done[i]
        if after < K:
            first = after // 128
            left = [done[i] for i, t in enumerate(active) if first <= t < 2]
            changed = [(i, t) for i, t in enumerate(active) if t >= first]
            update = tn(
                jnp.concatenate(left, 1), jnp.concatenate([done[i] for i, _ in changed], 1)
            )
            part = update[after - 128 * first : K - 128 * first]
            for s, (_, t) in enumerate(changed):
                aug[after:K, tile(t)] = aug[after:K, tile(t)] - part[:, tile(s)]

    block(0)
    block(1)

    pltpu.make_async_copy(q_recv, q_recv, qr_sem).wait()
    q_row = jnp.sum(q_recv[...], axis=0)
    step_coef = jnp.sum(coef_scr[...] * q_row, axis=1, keepdims=True)
    for c in range(6):
        joined = jnp.concatenate([u[c, M:, :], w[c], u[c, :M, :]], 0)
        disp_send[c] = disp_send[c] + jnp.sum(joined * step_coef, axis=0, keepdims=True)
        next_disp[c : c + 1, :] = disp_send[c]

    def table_copy(p):
        return remote(disp_send, row(table_own, chip), ts_sem, tr_sem, 2 * p + core)

    other_chips(lambda p: table_copy(p).start(), UNROLL)
    pltpu.make_async_copy(disp_send, row(table_own, chip), tr_sem).start()

    for b in range(2, K // NB):
        block(b)

    upper = jnp.where(iota((K, 256), 1) >= iota((K, 256), 0), aug[:, 0:256], 0.0)
    mix_u[...] = nn(upper[:, :K], change)
    mix_z[...] = aug[:, 256:512]

    gram_blocks(lambda b, slot, p: gram_copy(b, slot, p).wait_send(), None)
    reducing(lambda slot, b: others(lambda p: share_copy(slot, b, p).wait_send()))
    pair_copy.wait_send()
    other_chips(lambda p: load_copy(p).wait_send())
    others(lambda p: q_copy(p).wait_send())

    pltpu.make_async_copy(table_own, table_own, tr_sem).wait()
    forward = remote(table_own, table_pair, fs_sem, fr_sem, partner)
    forward.start()

    def put(table, parity):
        for c in range(6):
            high, low = split(table[c])
            at = pl.ds(pl.multiple_of(c * n + parity * half, half), half)
            table_hi[at, :] = high
            table_lo[at, :] = low

    put(table_own, core)
    other_chips(lambda p: table_copy(p).wait_send())
    forward.wait_recv()
    put(table_pair, 1 - core)
    forward.wait_send()


def finish_kernel(
    n, owner, target, table_hi, table_lo, mix_u, mix_z, u_any, z_any, v_any, w_any,
    u_out, z_out, wetted, u, z, v, w, u_buf, z_buf, in_sem, sem,
):
    loads = [
        pltpu.make_async_copy(src, dst, in_sem.at[i])
        for i, (src, dst) in enumerate(((u_any, u), (z_any, z), (v_any, v), (w_any, w)))
    ]
    for copy in loads:
        copy.start()
    half = n // 2
    faces = wetted.shape[1]
    chunk = min(GATHER_CHUNK, faces // 2)
    left = jnp.concatenate([table_hi[...], table_lo[...]], 1)

    def gather(i, carry):
        at = pl.ds(pl.multiple_of(i * chunk, chunk), chunk)
        name = owner[:, at]
        place = (name & 1) * half + (name >> 1)
        at_owner = iota((n, chunk), 0) == place
        at_point = (iota((BLK, chunk), 0) == target[:, at]).astype(F32).astype(BF16)
        right = jnp.concatenate([at_point, at_point], 0)
        values = lax.dot_general(left, right, (((1,), (0,)), ((), ())), preferred_element_type=F32)
        rows = [
            jnp.sum(jnp.where(at_owner, values[c * n : (c + 1) * n], 0.0), axis=0, keepdims=True)
            for c in range(6)
        ]
        wetted[:, at] = jnp.concatenate(rows, 0)
        return carry

    steps = faces // chunk
    lax.fori_loop(0, steps // 2, gather, 0)

    for copy in loads:
        copy.wait()
    left_u = mix_u[:, :ROWS]
    left_z = mix_z[:, :K]
    for c in range(6):
        u_buf[c] = nn(left_u, jnp.concatenate([u[c, M:, :], w[c], u[c, :M, :]], 0))
        z_buf[c] = nn(left_z, jnp.concatenate([z[c, M:, :], v[c]], 0))
    u_copy = pltpu.make_async_copy(u_buf, u_out, sem.at[0])
    z_copy = pltpu.make_async_copy(z_buf, z_out, sem.at[1])
    u_copy.start()
    z_copy.start()

    lax.fori_loop(steps // 2, steps, gather, 0)
    u_copy.wait()
    z_copy.wait()


def on_device(n_g, n_r, force_rows, owners, target, rbf_blocks, displacement, u_basis, z_basis, v_new, w_new):
    n = n_g * n_r
    half = n // 2
    faces = force_rows.shape[1]
    reducers = min(n, GBLK)
    slots = -(-GBLK // reducers)
    owner = owners.reshape(1, faces)
    point = target.reshape(1, faces)
    u, z, v, w = (x.transpose(1, 0, 2) for x in (u_basis, z_basis, v_new, w_new))
    vmem = pl.BlockSpec(memory_space=pltpu.VMEM)
    away = pl.BlockSpec(memory_space=pl.ANY)
    dma = pltpu.SemaphoreType.DMA
    table_hi, table_lo, mix_u, mix_z, next_disp = pl.pallas_call(
        functools.partial(exchange_kernel, n_g, n_r),
        out_shape=(
            jax.ShapeDtypeStruct((6 * n, BLK), BF16),
            jax.ShapeDtypeStruct((6 * n, BLK), BF16),
            jax.ShapeDtypeStruct((K, 256), F32),
            jax.ShapeDtypeStruct((K, 256), F32),
            jax.ShapeDtypeStruct((6, BLK), F32),
        ),
        in_specs=[vmem] * 3 + [away] * 6,
        out_specs=(vmem,) * 5,
        scratch_shapes=[
            pltpu.VMEM((BLK, BLK), F32),
            pltpu.VMEM((6, BLK), F32),
            pltpu.VMEM((6, K, BLK), F32),
            pltpu.VMEM((6, K, BLK), F32),
            pltpu.VMEM((6, M, BLK), F32),
            pltpu.VMEM((6, M, BLK), F32),
            pltpu.VMEM((GBLK, 8, 256), F32),
            pltpu.VMEM((slots, n, 8, 256), F32),
            pltpu.VMEM((slots, 8, 256), F32),
            pltpu.VMEM((GBLK, 8, 256), F32),
            pltpu.VMEM((6, half, BLK), F32),
            pltpu.VMEM((6, half, BLK), F32),
            pltpu.VMEM((6, half, BLK), F32),
            pltpu.VMEM((6, half, BLK), F32),
            pltpu.VMEM((1, 256), F32),
            pltpu.VMEM((n, 1, 256), F32),
            pltpu.VMEM((6, 1, BLK), F32),
            pltpu.VMEM((6, half, BLK), F32),
            pltpu.VMEM((6, half, BLK), F32),
            pltpu.VMEM((K, 512), F32),
            pltpu.VMEM((ROWS, 256), F32),
            dma((6,)),
            dma,
            dma((slots,)),
        ]
        + [dma] * 12,
        compiler_params=pltpu.CompilerParams(collective_id=0, has_side_effects=True),
        name="exchange",
    )(force_rows, owner, point, rbf_blocks[0], displacement, u, z, v, w)
    u_out, z_out, wetted = pl.pallas_call(
        functools.partial(finish_kernel, n),
        out_shape=(
            jax.ShapeDtypeStruct((6, K, BLK), F32),
            jax.ShapeDtypeStruct((6, K, BLK), F32),
            jax.ShapeDtypeStruct((6, faces), F32),
        ),
        in_specs=[vmem] * 6 + [away] * 4,
        out_specs=(away, away, vmem),
        scratch_shapes=[
            pltpu.VMEM((6, K, BLK), F32),
            pltpu.VMEM((6, K, BLK), F32),
            pltpu.VMEM((6, M, BLK), F32),
            pltpu.VMEM((6, M, BLK), F32),
            pltpu.VMEM((6, K, BLK), F32),
            pltpu.VMEM((6, K, BLK), F32),
            dma((4,)),
            dma((2,)),
        ],
        name="finish",
    )(owner, point, table_hi, table_lo, mix_u, mix_z, u, z, v, w)
    return u_out.transpose(1, 0, 2), z_out.transpose(1, 0, 2), next_disp, wetted


def solution(mesh):
    return jax.shard_map(
        functools.partial(on_device, mesh.shape["group"], mesh.shape["rows"]),
        mesh=mesh,
        in_specs=(
            P(None, AXES),
            P(AXES, None),
            P(AXES),
            P(AXES, None, None),
            P(None, AXES),
            P(None, None, AXES),
            P(None, None, AXES),
            P(None, None, AXES),
            P(None, None, AXES),
        ),
        out_specs=(P(None, None, AXES), P(None, None, AXES), P(None, AXES), P(None, AXES)),
        check_vma=False,
    )
```

```python
import functools

import jax
import jax.numpy as jnp
from jax import lax
from jax.experimental import pallas as pl
from jax.experimental.pallas import tpu as pltpu
from jax.sharding import PartitionSpec as P

BLK = 256
K = 192
M = 32
KEEP = K - M
NB = 32
ROWS = K + M
SHARES = ROWS // 2
FACE_CHUNK = 2048
GATHER_CHUNK = 2048
UNROLL = 8

MESH = pl.DeviceIdType.MESH
F32 = jnp.float32
BF16 = jnp.bfloat16
AXES = ("group", "rows")


def iota(shape, dim):
    return lax.broadcasted_iota(jnp.int32, shape, dim)


def dot(a, b, dims):
    return lax.dot_general(
        a, b, (dims, ((), ())), precision=lax.Precision.HIGHEST, preferred_element_type=F32
    )


def nn(a, b):
    return dot(a, b, ((1,), (0,)))


def nt(a, b):
    return dot(a, b, ((1,), (1,)))


def tn(a, b):
    return dot(a, b, ((0,), (0,)))


def split(x):
    high = x.astype(BF16)
    return high, (x - high.astype(F32)).astype(BF16)


def eliminate(tiles, first):
    rows = iota((NB, 128), 0)
    tiles = list(tiles)
    base = first // 128
    for j in range(0, NB, 4):
        lane = first % 128 + j
        pivot_tile = tiles[base]
        c = [jnp.broadcast_to(pivot_tile[:, lane + i : lane + i + 1], (NB, 128)) for i in range(4)]
        a = {
            (i, k): jnp.broadcast_to(c[k][j + i : j + i + 1, :], (NB, 128))
            for i in range(4)
            for k in range(i, 4)
        }
        p0 = 1.0 / a[0, 0]
        l1, l2, l3 = a[0, 1] * p0, a[0, 2] * p0, a[0, 3] * p0
        b11, b12, b13 = a[1, 1] - l1 * a[0, 1], a[1, 2] - l1 * a[0, 2], a[1, 3] - l1 * a[0, 3]
        b22, b23, b33 = a[2, 2] - l2 * a[0, 2], a[2, 3] - l2 * a[0, 3], a[3, 3] - l3 * a[0, 3]
        p1 = 1.0 / b11
        l21, l31 = b12 * p1, b13 * p1
        b22, b23, b33 = b22 - l21 * b12, b23 - l21 * b13, b33 - l31 * b13
        p2 = 1.0 / b22
        l32 = b23 * p2
        p3 = 1.0 / (b33 - l32 * b23)
        m0 = jnp.where(rows > j, c[0] * p0, 0.0)
        m1 = jnp.where(rows > j + 1, (c[1] - m0 * a[0, 1]) * p1, 0.0)
        m2 = jnp.where(rows > j + 2, (c[2] - m0 * a[0, 2] - m1 * b12) * p2, 0.0)
        m3 = jnp.where(rows > j + 3, (c[3] - m0 * a[0, 3] - m1 * b13 - m2 * b23) * p3, 0.0)
        m2 = m2 - m3 * l32
        m1 = m1 - m2 * l21 - m3 * l31
        m0 = m0 - m1 * l1 - m2 * l2 - m3 * l3
        for t, tile in enumerate(tiles):
            r = [tile[j + i : j + i + 1, :] for i in range(4)]
            tiles[t] = tile - (m0 * r[0] + m1 * r[1]) - (m2 * r[2] + m3 * r[3])
    own = iota((NB, 128), 1) == first % 128 + rows
    pivots = jnp.sum(jnp.where(own, tiles[base], 0.0), axis=1, keepdims=True)
    scale = lax.rsqrt(pivots)
    return [tile * scale for tile in tiles]
def exchange_kernel(
    n_g, n_r,
    force, owner, target, rbf_any, disp_any, u_any, z_any, v_any, w_any,
    table_hi, table_lo, mix_u, mix_z, next_disp,
    rbf, disp, u, z, v, w,
    gram_send, gram_recv, gram_sum, gram_all,
    load_pair, load_own, pair_recv, load_recv, q_send, q_recv, disp_send, table_own, table_pair,
    aug, coef_scr,
    in_sem, gs_sem, gr_sem, ga_send_sem, ga_sem, ps_sem, pr_sem, ls_sem, lr_sem,
    qs_sem, qr_sem, ts_sem, tr_sem, fs_sem, fr_sem,
):
    n = n_g * n_r
    half = n // 2
    me = lax.axis_index("group") * n_r + lax.axis_index("rows")
    chip, core = me // 2, lax.rem(me, 2)
    dof_total = 6 * BLK * n

    def device(p):
        return (p // n_r, lax.rem(p, n_r))

    def others(body, unroll=1):
        def step(k, carry):
            body(lax.rem(me + k, n))
            return carry

        lax.fori_loop(1, n, step, 0, unroll=unroll)

    def other_chips(body, unroll=1):
        def step(k, carry):
            body(lax.rem(chip + k, half))
            return carry

        lax.fori_loop(1, half, step, 0, unroll=unroll)

    def remote(src, dst, send, recv, p):
        return pltpu.make_async_remote_copy(
            src_ref=src, dst_ref=dst, send_sem=send, recv_sem=recv,
            device_id=device(p), device_id_type=MESH,
        )

    loads = [
        pltpu.make_async_copy(src, dst, in_sem.at[i])
        for i, (src, dst) in enumerate(
            ((z_any, z), (v_any, v), (rbf_any, rbf), (disp_any, disp), (u_any, u), (w_any, w))
        )
    ]
    for copy in loads:
        copy.start()
    barrier = pltpu.get_barrier_semaphore()
    others(
        lambda p: pl.semaphore_signal(barrier, inc=1, device_id=device(p), device_id_type=MESH),
        UNROLL,
    )

    loads[0].wait()
    loads[1].wait()
    gram = jnp.zeros((ROWS, ROWS), F32)
    for c in range(6):
        joined = jnp.concatenate([z[c, M:, :], v[c], z[c, :M, :]], 0)
        gram = gram + nt(joined, joined)
    gram = gram * (1.0 / dof_total)
    gram = jnp.concatenate([gram, jnp.zeros((ROWS, 256 - ROWS), F32)], 1)
    gram_send[...] = gram.reshape(2, SHARES, 256)

    faces = force.shape[1]
    chunk = min(FACE_CHUNK, faces)

    def scatter_to(load, parity):
        def scatter(i, carry):
            at = pl.ds(pl.multiple_of(i * chunk, chunk), chunk)
            named = iota((half, chunk), 0) * 2 + parity
            at_owner = (named == owner[:, at]).astype(F32).astype(BF16)
            at_point = (iota((BLK, chunk), 0) == target[:, at]).astype(F32).astype(BF16)
            high, low = split(force[:, at])
            left = jnp.concatenate(
                [
                    jnp.concatenate([at_owner * high[c : c + 1], at_owner * low[c : c + 1]], 1)
                    for c in range(6)
                ],
                0,
            )
            right = jnp.concatenate([at_point, at_point], 1)
            add = lax.dot_general(
                left, right, (((1,), (1,)), ((), ())), preferred_element_type=F32
            )
            load[...] += add.reshape(6, half, BLK)
            return carry

        load[...] = jnp.zeros_like(load)
        lax.fori_loop(0, faces // chunk, scatter, 0)

    scatter_to(load_pair, 1 - core)

    pl.semaphore_wait(barrier, n - 1)

    def row(ref, p):
        return ref.at[:, pl.ds(p, 1), :]

    def gram_copy(p):
        return remote(row(gram_send, p), row(gram_recv, me), gs_sem, gr_sem, p)

    def to_shares(body, unroll=1):
        def guarded(p):
            @pl.when(p < SHARES)
            def _():
                body(p)

        others(guarded, unroll)

    to_shares(lambda p: gram_copy(p).start(), UNROLL)

    @pl.when(me < SHARES)
    def _():
        pltpu.make_async_copy(row(gram_send, me), row(gram_recv, me), gr_sem).start()

    partner = 2 * chip + 1 - core
    pair_copy = remote(load_pair, pair_recv, ps_sem, pr_sem, partner)
    pair_copy.start()

    scatter_to(load_own, core)

    pair_copy.wait_recv()
    load_own[...] += pair_recv[...]

    def load_copy(p):
        return remote(row(load_own, p), row(load_recv, chip), ls_sem, lr_sem, 2 * p + core)

    other_chips(lambda p: load_copy(p).start(), UNROLL)
    pltpu.make_async_copy(row(load_own, chip), row(load_recv, chip), lr_sem).start()

    def share_copy(p):
        return remote(gram_sum, row(gram_all, me), ga_send_sem, ga_sem, p)

    @pl.when(me < SHARES)
    def _():
        pltpu.make_async_copy(gram_recv, gram_recv, gr_sem).wait()
        for i in range(2):
            gram_sum[i] = jnp.sum(gram_recv[i], axis=0, keepdims=True)
        others(lambda p: share_copy(p).start(), UNROLL)
        pltpu.make_async_copy(gram_sum, row(gram_all, me), ga_sem).start()

    for copy in loads[2:]:
        copy.wait()

    pltpu.make_async_copy(load_recv, load_recv, lr_sem).wait()
    point_load = jnp.concatenate(
        [jnp.sum(load_recv[c], axis=0, keepdims=True) for c in range(6)], 0
    )
    response = nn(point_load, rbf[...])
    residual = response - disp[...]
    disp_send[...] = response.reshape(6, 1, BLK)
    weighted = jnp.zeros((K, BLK), F32)
    for c in range(6):
        kept = jnp.concatenate([z[c, M:, :], v[c]], 0)
        weighted = weighted + kept * residual[c : c + 1]
    q_column = jnp.sum(weighted, axis=1, keepdims=True) * (1.0 / dof_total)
    diagonal = iota((K, 256), 0) == iota((K, 256), 1)
    q_send[...] = jnp.sum(jnp.where(diagonal, q_column, 0.0), axis=0, keepdims=True)

    def q_copy(p):
        return remote(q_send, q_recv.at[me], qs_sem, qr_sem, p)

    others(lambda p: q_copy(p).start(), UNROLL)
    pltpu.make_async_copy(q_send, q_recv.at[me], qr_sem).start()

    pltpu.make_async_copy(gram_all, gram_all, ga_sem).wait()
    total = gram_all[...].reshape(ROWS, 256)

    lane32 = iota((NB, 128), 1)
    row32 = iota((NB, 128), 0)
    middle = (lane32 >= 32) & (lane32 < 64)
    start = jnp.where(middle, total[KEEP:K, 128:], jnp.where(lane32 - 64 == row32, 1.0, 0.0))
    factor = pltpu.roll(eliminate([start], 32)[0], 96, 1)
    factor = jnp.where(middle, factor, 0.0)
    inverse = tn(factor, factor)
    scaled = nn(total[:, 128:], inverse)

    lanes = iota((ROWS, 256), 1)
    index = iota((ROWS, 256), 0)
    new_lane = (lanes >= KEEP) & (lanes < K)
    new_row = (index >= KEEP) & (index < K)
    scaled = jnp.concatenate([jnp.zeros((ROWS, 128), F32), scaled], 1)
    inverse_rows = jnp.concatenate(
        [jnp.zeros((KEEP, 128), F32), inverse[32:64], jnp.zeros((M, 128), F32)], 0
    )
    inverse_full = jnp.concatenate([jnp.zeros((ROWS, 128), F32), inverse_rows], 1)
    unit = jnp.where(lanes == index, 1.0, 0.0)
    matrix = jnp.where(new_lane, jnp.where(new_row, inverse_full, scaled), total)
    matrix = jnp.where(lanes < K, matrix, 0.0)
    extra = jnp.where(new_lane, inverse_full, unit)
    aug[:, 0:256] = matrix[:K]
    aug[:, 256:512] = extra[:K]
    coef_scr[...] = jnp.where(
        new_lane,
        jnp.where(new_row, inverse_full, -scaled),
        jnp.where(lanes < KEEP, unit, 0.0),
    )
    change = jnp.where(lanes == index, 1.0, jnp.where(new_row & (lanes < ROWS), -total, 0.0))
    change = jnp.where(new_row & new_lane, unit, change)[:K]

    def tile(t):
        return slice(t * 128, t * 128 + 128)

    def block(b):
        r0, after = b * NB, b * NB + NB
        rows = slice(r0, after)
        active = [0, 1, 2] if after <= 128 else [1, 2, 3]
        done = eliminate([aug[rows, tile(t)] for t in active], r0 - 128 * active[0])
        lane = iota((NB, 128), 1)
        for i, t in enumerate(active):
            if t < 2:
                done[i] = jnp.where(lane + t * 128 < r0, 0.0, done[i])
            aug[rows, tile(t)] = done[i]
        if after < K:
            first = after // 128
            left = [done[i] for i, t in enumerate(active) if first <= t < 2]
            changed = [(i, t) for i, t in enumerate(active) if t >= first]
            update = tn(
                jnp.concatenate(left, 1), jnp.concatenate([done[i] for i, _ in changed], 1)
            )
            part = update[after - 128 * first : K - 128 * first]
            for s, (_, t) in enumerate(changed):
                aug[after:K, tile(t)] = aug[after:K, tile(t)] - part[:, tile(s)]

    block(0)

    pltpu.make_async_copy(q_recv, q_recv, qr_sem).wait()
    q_row = jnp.sum(q_recv[...], axis=0)
    step_coef = jnp.sum(coef_scr[...] * q_row, axis=1, keepdims=True)
    for c in range(6):
        joined = jnp.concatenate([u[c, M:, :], w[c], u[c, :M, :]], 0)
        disp_send[c] = disp_send[c] + jnp.sum(joined * step_coef, axis=0, keepdims=True)
        next_disp[c : c + 1, :] = disp_send[c]

    def table_copy(p):
        return remote(disp_send, row(table_own, chip), ts_sem, tr_sem, 2 * p + core)

    other_chips(lambda p: table_copy(p).start(), UNROLL)
    pltpu.make_async_copy(disp_send, row(table_own, chip), tr_sem).start()

    for b in range(1, K // NB):
        block(b)

    upper = jnp.where(iota((K, 256), 1) >= iota((K, 256), 0), aug[:, 0:256], 0.0)
    mix_u[...] = nn(upper[:, :K], change)
    mix_z[...] = aug[:, 256:512]

    to_shares(lambda p: gram_copy(p).wait_send())

    @pl.when(me < SHARES)
    def _():
        others(lambda p: share_copy(p).wait_send())

    pair_copy.wait_send()
    other_chips(lambda p: load_copy(p).wait_send())
    others(lambda p: q_copy(p).wait_send())

    pltpu.make_async_copy(table_own, table_own, tr_sem).wait()
    forward = remote(table_own, table_pair, fs_sem, fr_sem, partner)
    forward.start()

    def put(table, parity):
        for c in range(6):
            high, low = split(table[c])
            at = pl.ds(pl.multiple_of(c * n + parity * half, half), half)
            table_hi[at, :] = high
            table_lo[at, :] = low

    put(table_own, core)
    other_chips(lambda p: table_copy(p).wait_send())
    forward.wait_recv()
    put(table_pair, 1 - core)
    forward.wait_send()


def finish_kernel(
    n, owner, target, table_hi, table_lo, mix_u, mix_z, disp_in, u_any, z_any, v_any, w_any,
    u_out, z_out, disp_out, wetted, u, z, v, w, u_buf, z_buf, in_sem, sem,
):
    loads = [
        pltpu.make_async_copy(src, dst, in_sem.at[i])
        for i, (src, dst) in enumerate(((u_any, u), (z_any, z), (v_any, v), (w_any, w)))
    ]
    for copy in loads:
        copy.start()
    disp_out[...] = disp_in[...]
    half = n // 2
    faces = wetted.shape[1]
    chunk = min(GATHER_CHUNK, faces // 2)
    left = jnp.concatenate([table_hi[...], table_lo[...]], 1)

    def gather(i, carry):
        at = pl.ds(pl.multiple_of(i * chunk, chunk), chunk)
        name = owner[:, at]
        place = (name & 1) * half + (name >> 1)
        at_owner = iota((n, chunk), 0) == place
        at_point = (iota((BLK, chunk), 0) == target[:, at]).astype(F32).astype(BF16)
        right = jnp.concatenate([at_point, at_point], 0)
        values = lax.dot_general(left, right, (((1,), (0,)), ((), ())), preferred_element_type=F32)
        rows = [
            jnp.sum(jnp.where(at_owner, values[c * n : (c + 1) * n], 0.0), axis=0, keepdims=True)
            for c in range(6)
        ]
        wetted[:, at] = jnp.concatenate(rows, 0)
        return carry

    steps = faces // chunk
    lax.fori_loop(0, steps // 2, gather, 0)

    for copy in loads:
        copy.wait()
    left_u = mix_u[:, :ROWS]
    left_z = mix_z[:, :K]
    for c in range(6):
        u_buf[c] = nn(left_u, jnp.concatenate([u[c, M:, :], w[c], u[c, :M, :]], 0))
        z_buf[c] = nn(left_z, jnp.concatenate([z[c, M:, :], v[c]], 0))
    u_copy = pltpu.make_async_copy(u_buf, u_out, sem.at[0])
    z_copy = pltpu.make_async_copy(z_buf, z_out, sem.at[1])
    u_copy.start()
    z_copy.start()

    lax.fori_loop(steps // 2, steps, gather, 0)
    u_copy.wait()
    z_copy.wait()


def on_device(n_g, n_r, force_rows, owners, target, rbf_blocks, displacement, u_basis, z_basis, v_new, w_new):
    n = n_g * n_r
    half = n // 2
    faces = force_rows.shape[1]
    owner = owners.reshape(1, faces)
    point = target.reshape(1, faces)
    u, z, v, w = (x.transpose(1, 0, 2) for x in (u_basis, z_basis, v_new, w_new))
    vmem = pl.BlockSpec(memory_space=pltpu.VMEM)
    away = pl.BlockSpec(memory_space=pl.ANY)
    dma = pltpu.SemaphoreType.DMA
    table_hi, table_lo, mix_u, mix_z, next_disp = pl.pallas_call(
        functools.partial(exchange_kernel, n_g, n_r),
        out_shape=(
            jax.ShapeDtypeStruct((6 * n, BLK), BF16),
            jax.ShapeDtypeStruct((6 * n, BLK), BF16),
            jax.ShapeDtypeStruct((K, 256), F32),
            jax.ShapeDtypeStruct((K, 256), F32),
            jax.ShapeDtypeStruct((6, BLK), F32),
        ),
        in_specs=[vmem] * 3 + [away] * 6,
        out_specs=(vmem,) * 5,
        scratch_shapes=[
            pltpu.VMEM((BLK, BLK), F32),
            pltpu.VMEM((6, BLK), F32),
            pltpu.VMEM((6, K, BLK), F32),
            pltpu.VMEM((6, K, BLK), F32),
            pltpu.VMEM((6, M, BLK), F32),
            pltpu.VMEM((6, M, BLK), F32),
            pltpu.VMEM((2, SHARES, 256), F32),
            pltpu.VMEM((2, n, 256), F32),
            pltpu.VMEM((2, 1, 256), F32),
            pltpu.VMEM((2, SHARES, 256), F32),
            pltpu.VMEM((6, half, BLK), F32),
            pltpu.VMEM((6, half, BLK), F32),
            pltpu.VMEM((6, half, BLK), F32),
            pltpu.VMEM((6, half, BLK), F32),
            pltpu.VMEM((1, 256), F32),
            pltpu.VMEM((n, 1, 256), F32),
            pltpu.VMEM((6, 1, BLK), F32),
            pltpu.VMEM((6, half, BLK), F32),
            pltpu.VMEM((6, half, BLK), F32),
            pltpu.VMEM((K, 512), F32),
            pltpu.VMEM((ROWS, 256), F32),
            dma((6,)),
        ]
        + [dma] * 14,
        compiler_params=pltpu.CompilerParams(collective_id=0, has_side_effects=True),
        name="exchange",
    )(force_rows, owner, point, rbf_blocks[0], displacement, u, z, v, w)
    u_out, z_out, next_disp, wetted = pl.pallas_call(
        functools.partial(finish_kernel, n),
        out_shape=(
            jax.ShapeDtypeStruct((6, K, BLK), F32),
            jax.ShapeDtypeStruct((6, K, BLK), F32),
            jax.ShapeDtypeStruct((6, BLK), F32),
            jax.ShapeDtypeStruct((6, faces), F32),
        ),
        in_specs=[vmem] * 7 + [away] * 4,
        out_specs=(away, away, vmem, vmem),
        scratch_shapes=[
            pltpu.VMEM((6, K, BLK), F32),
            pltpu.VMEM((6, K, BLK), F32),
            pltpu.VMEM((6, M, BLK), F32),
            pltpu.VMEM((6, M, BLK), F32),
            pltpu.VMEM((6, K, BLK), F32),
            pltpu.VMEM((6, K, BLK), F32),
            dma((4,)),
            dma((2,)),
        ],
        name="finish",
    )(owner, point, table_hi, table_lo, mix_u, mix_z, next_disp, u, z, v, w)
    return u_out.transpose(1, 0, 2), z_out.transpose(1, 0, 2), next_disp, wetted


def solution(mesh):
    return jax.shard_map(
        functools.partial(on_device, mesh.shape["group"], mesh.shape["rows"]),
        mesh=mesh,
        in_specs=(
            P(None, AXES),
            P(AXES, None),
            P(AXES),
            P(AXES, None, None),
            P(None, AXES),
            P(None, None, AXES),
            P(None, None, AXES),
            P(None, None, AXES),
            P(None, None, AXES),
        ),
        out_specs=(P(None, None, AXES), P(None, None, AXES), P(None, AXES), P(None, AXES)),
        check_vma=False,
    )
```
